32 devices in a mesh: seq: 2 (over y), row: 4 (over x, core), col: 4 (over z).
Axes of the slice: x: 2, y: 2, z: 4, core: 2. Of those that a mesh axis runs over, the one named last changes fastest.
Arguments:
- tokens: bfloat16 [4096, 5376], P(('seq', 'row'), 'col'), may hold values from -6 to 6
- w_query: bfloat16 [5376, 4096], P(('seq', 'row'), 'col'), may hold values from -0.078125 to 0.078125
- key_weight: bfloat16 [5376, 2048], P(('seq', 'row'), 'col'), may hold values from -0.078125 to 0.078125
- value_weight: bfloat16 [5376, 2048], P(('seq', 'row'), 'col'), may hold values from -0.078125 to 0.078125
- w_output: bfloat16 [4096, 5376], P(('seq', 'row'), 'col'), may hold values from -0.09375 to 0.09375
- query_gain: float32 [128], replicated, may hold values from 0.5 to 8
- key_gain: float32 [128], replicated, may hold values from 0.5 to 8
Outputs:
- attended: bfloat16 [4096, 5376], P(('seq', 'row'), 'col')
The draws below stay inside these ranges and needn't reach their ends.
All inputs are finite; a program needn't handle non-finite values.
Results may differ from the reference program's by a relative error of at most 0.0085.
The reference program's roundings to bfloat16 on the way count: a program that leaves them out, or rounds other values in their place, can miss the bound.
Values may be sent and summed in bfloat16 or wider, within the bound.
A program may use at most 128 MiB of HBM per device.

```python
import jax
import jax.numpy as jnp
from jax import lax

MODEL_WIDTH = 5376
HQ = 32
KEY_VALUE_HEADS = 16
HEAD_SIZE = 128
WINDOW_KEYS = 1024
TOK_DEV = 512
TOKENS = 4096


def draw_query_gain(key, part):
    local = jax.random.fold_in(key, 11)
    return jax.random.uniform(local, (HEAD_SIZE,), jnp.float32, 0.5, 1.5)


def draw_key_gain(key, part):
    local = jax.random.fold_in(key, 12)
    return jax.random.uniform(local, (HEAD_SIZE,), jnp.float32, 0.5, 1.5)


def block_levels(own_key, extent, pieces, smallest, high):
    level = 1.0
    for axis_at, shards_of in pieces:
        draws = jax.random.uniform(jax.random.fold_in(jax.random.fold_in(own_key, 6), axis_at), (shards_of,), jnp.float32, smallest / len(pieces), high / len(pieces))
        level = level * jnp.repeat(jnp.exp(draws), extent[axis_at] // shards_of).reshape((-1,) + (1,) * (len(extent) - 1 - axis_at))
    return level


def centred(stream_key, shape, width, most, shards=(), kind=jnp.bfloat16):
    drawn = width * jax.random.normal(stream_key, shape, jnp.float32)
    if shards:
        drawn = drawn * block_levels(stream_key, shape, shards, -0.22, 0.18)
    return jnp.clip(drawn, -most, most).astype(kind)


def setup_inputs(seed: int = 0) -> dict:
    keys = jax.random.split(jax.random.key(seed), 8)
    return {
        "tokens": centred(keys[0], (TOKENS, MODEL_WIDTH), 1.0, 6.0, ((0, 8), (1, 4))),
        "w_query": centred(keys[1], (MODEL_WIDTH, HQ * HEAD_SIZE), MODEL_WIDTH ** -0.5, 0.078125, ((0, 8), (1, 4))),
        "key_weight": centred(keys[2], (MODEL_WIDTH, KEY_VALUE_HEADS * HEAD_SIZE), MODEL_WIDTH ** -0.5, 0.078125, ((0, 8), (1, 4))),
        "value_weight": centred(keys[3], (MODEL_WIDTH, KEY_VALUE_HEADS * HEAD_SIZE), MODEL_WIDTH ** -0.5, 0.078125, ((0, 8), (1, 4))),
        "w_output": centred(keys[4], (HQ * HEAD_SIZE, MODEL_WIDTH), (HQ * HEAD_SIZE) ** -0.5, 0.09375, ((0, 8), (1, 4))),
        "query_gain": draw_query_gain(jax.random.fold_in(keys[7], 71), 0),
        "key_gain": draw_key_gain(jax.random.fold_in(keys[7], 71), 0),
    }


query_scale = 168.0 ** (-0.5)

def head_norm(block, gain):
    mean_square = lax.optimization_barrier(jnp.mean(block * block, axis=-1, keepdims=True))
    return block * lax.rsqrt(mean_square + 1e-06) * gain

def rotate(block, positions):
    half = block.shape[-1] // 2
    freqs = 10000.0 ** (-(jnp.arange(half, dtype=jnp.float32) * 2.0 / block.shape[-1]))
    angles = positions.astype(jnp.float32)[:, None] * freqs[None, :]
    cosine = jnp.cos(angles)[:, None, :]
    sine = jnp.sin(angles)[:, None, :]
    first = block[..., :half]
    second = block[..., half:]
    return jnp.concatenate([first * cosine - second * sine, second * cosine + first * sine], axis=-1)

def attend(queries, key_states, value_states, qpos, kpos):
    rows = queries.shape[0]
    kv_heads = key_states.shape[1]
    grouped = queries.astype(jnp.float32).reshape(rows, kv_heads, 2, HEAD_SIZE)
    scores = jnp.einsum('bhgd,khd->hgbk', grouped, key_states.astype(jnp.float32)) * query_scale
    gap = qpos[:, None] - kpos[None, :]
    valid = (kpos[None, :] >= 0) & (gap >= 0) & (gap < WINDOW_KEYS)
    scores = jnp.where(valid[None, None], scores, -1e+30)
    top = lax.optimization_barrier(jnp.max(scores, axis=-1, keepdims=True))
    weights = jnp.exp(scores - top)
    weights = (weights / lax.optimization_barrier(jnp.sum(weights, axis=-1, keepdims=True))).astype(jnp.bfloat16)
    mixed = jnp.einsum('hgbk,khd->bhgd', weights.astype(jnp.float32), value_states.astype(jnp.float32))
    return mixed.astype(jnp.bfloat16).reshape(rows, kv_heads * 2 * HEAD_SIZE)

def reference(tokens, w_query, key_weight, value_weight, w_output, query_gain, key_gain):
    total_length = tokens.shape[0]
    positions = jnp.arange(total_length, dtype=jnp.int32)
    proj_q = jnp.dot(tokens, w_query, preferred_element_type=jnp.float32).reshape(total_length, HQ, HEAD_SIZE)
    projected_key = jnp.dot(tokens, key_weight, preferred_element_type=jnp.float32).reshape(total_length, KEY_VALUE_HEADS, HEAD_SIZE)
    value_states = jnp.dot(tokens, value_weight, preferred_element_type=jnp.float32).astype(jnp.bfloat16).reshape(total_length, KEY_VALUE_HEADS, HEAD_SIZE)
    queries = rotate(head_norm(proj_q, query_gain), positions).astype(jnp.bfloat16)
    key_states = rotate(head_norm(projected_key, key_gain), positions).astype(jnp.bfloat16)
    block = TOK_DEV
    count = total_length // block
    key_padded_rows = jnp.concatenate([jnp.zeros((WINDOW_KEYS, KEY_VALUE_HEADS, HEAD_SIZE), jnp.bfloat16), key_states], axis=0)
    value_padded_rows = jnp.concatenate([jnp.zeros((WINDOW_KEYS, KEY_VALUE_HEADS, HEAD_SIZE), jnp.bfloat16), value_states], axis=0)

    def one_block(index):
        start = (index * block).astype(jnp.int32)
        query_rows = lax.dynamic_slice_in_dim(queries, start, block, 0)
        key_rows = lax.dynamic_slice_in_dim(key_padded_rows, start, block + WINDOW_KEYS, 0)
        value_rows = lax.dynamic_slice_in_dim(value_padded_rows, start, block + WINDOW_KEYS, 0)
        qpos = start + jnp.arange(block, dtype=jnp.int32)
        kpos = start - WINDOW_KEYS + jnp.arange(block + WINDOW_KEYS, dtype=jnp.int32)
        return attend(query_rows, key_rows, value_rows, qpos, kpos)
    mixed = lax.map(one_block, jnp.arange(count, dtype=jnp.int32)).reshape(total_length, HQ * HEAD_SIZE)
    return jnp.dot(mixed, w_output, preferred_element_type=jnp.float32).astype(jnp.bfloat16)
```

```python
import jax
import jax.numpy as jnp
from jax import lax
from jax.experimental import pallas as pl
from jax.experimental.pallas import tpu as pltpu
from jax.sharding import PartitionSpec as P

HEAD_SIZE = 128
WINDOW_KEYS = 1024


query_scale = 168.0 ** (-0.5)


def shifted(block, axis, distance):
    devices = range(lax.axis_size(axis))
    route = [(i - distance, i) for i in devices if i - distance in devices]
    return lax.ppermute(block, axis, route)


def head_norm(block, gain):
    mean_square = jnp.mean(block * block, axis=-1, keepdims=True)
    return block * lax.rsqrt(mean_square + 1e-06) * gain


def rotate(block, positions):
    half = block.shape[-1] // 2
    freqs = 10000.0 ** (-(jnp.arange(half, dtype=jnp.float32) * 2.0 / block.shape[-1]))
    angles = positions.astype(jnp.float32)[:, None] * freqs[None, :]
    cosine = jnp.cos(angles)[:, None, :]
    sine = jnp.sin(angles)[:, None, :]
    first = block[..., :half]
    second = block[..., half:]
    return jnp.concatenate(
        [first * cosine - second * sine, second * cosine + first * sine], axis=-1
    )


def attend(queries, key_states, value_states, qpos, kpos):
    rows = queries.shape[0]
    kv_heads = key_states.shape[1]
    grouped = queries.reshape(rows, kv_heads, 2, HEAD_SIZE)
    scores = (
        jnp.einsum("bhgd,khd->hgbk", grouped, key_states, preferred_element_type=jnp.float32)
        * query_scale
    )
    gap = qpos[:, None] - kpos[None, :]
    valid = (kpos[None, :] >= 0) & (gap >= 0) & (gap < WINDOW_KEYS)
    scores = jnp.where(valid[None, None], scores, -1e30)
    top = jnp.max(scores, axis=-1, keepdims=True)
    weights = jnp.exp(scores - top)
    weights = (weights / jnp.sum(weights, axis=-1, keepdims=True)).astype(jnp.bfloat16)
    mixed = jnp.einsum("hgbk,khd->bhgd", weights, value_states, preferred_element_type=jnp.float32)
    return mixed.astype(jnp.bfloat16).reshape(rows, kv_heads * 2 * HEAD_SIZE)


def shards(tokens, w_query, key_weight, value_weight, w_output, query_gain, key_gain):
    rows = tokens.shape[0]
    whole = lax.all_gather(tokens, "col", axis=1, tiled=True)
    columns = whole
    proj_q = jnp.dot(
        columns,
        lax.all_gather(w_query, ("seq", "row"), axis=0, tiled=True),
        preferred_element_type=jnp.float32,
    )
    projected_key = jnp.dot(
        columns,
        lax.all_gather(key_weight, ("seq", "row"), axis=0, tiled=True),
        preferred_element_type=jnp.float32,
    )
    proj_v = jnp.dot(
        columns,
        lax.all_gather(value_weight, ("seq", "row"), axis=0, tiled=True),
        preferred_element_type=jnp.float32,
    )
    base = lax.axis_index(("seq", "row")) * rows
    positions = base + jnp.arange(rows, dtype=jnp.int32)
    q_heads = proj_q.shape[1] // HEAD_SIZE
    kv_heads = projected_key.shape[1] // HEAD_SIZE
    queries = rotate(
        head_norm(proj_q.reshape(rows, q_heads, HEAD_SIZE), query_gain), positions
    ).astype(jnp.bfloat16)
    key_states = rotate(
        head_norm(projected_key.reshape(rows, kv_heads, HEAD_SIZE), key_gain), positions
    ).astype(jnp.bfloat16)
    key_flat = key_states.reshape(rows, kv_heads * HEAD_SIZE)
    value_flat = proj_v.astype(jnp.bfloat16)
    prior_one = shifted((key_flat, value_flat), ("seq", "row"), 1)
    prior_two = shifted((key_flat, value_flat), ("seq", "row"), 2)
    key_rows = jnp.concatenate([prior_two[0], prior_one[0], key_flat], axis=0).reshape(
        3 * rows, kv_heads, HEAD_SIZE
    )
    value_rows = jnp.concatenate([prior_two[1], prior_one[1], value_flat], axis=0).reshape(
        3 * rows, kv_heads, HEAD_SIZE
    )
    kpos = base - 2 * rows + jnp.arange(3 * rows, dtype=jnp.int32)
    mixed = attend(queries, key_rows, value_rows, positions, kpos)
    all_heads = lax.all_gather(mixed, "col", axis=1, tiled=True)
    columns = all_heads
    attended = jnp.dot(
        columns,
        lax.all_gather(w_output, ("seq", "row"), axis=0, tiled=True),
        preferred_element_type=jnp.float32,
    )
    return attended.astype(jnp.bfloat16)


MESH = pl.DeviceIdType.MESH
MIB = 1 << 20


class Place:
    def __init__(self):
        self.y = lax.axis_index("seq")
        row = lax.axis_index("row")
        self.x, self.c = row // 2, row % 2
        self.z = lax.axis_index("col")
        self.to_x = {"seq": self.y, "row": (1 - self.x) * 2 + self.c, "col": self.z}
        self.to_y = {"seq": 1 - self.y, "row": row, "col": self.z}
        self.to_c = {"seq": self.y, "row": self.x * 2 + 1 - self.c, "col": self.z}
        self.up = {"seq": self.y, "row": row, "col": self.z + 1}
        self.down = {"seq": self.y, "row": row, "col": self.z - 1}
        self.chip = self.y * 2 + self.x
        self.chip_x = self.y * 2 + 1 - self.x
        self.chip_y = (1 - self.y) * 2 + self.x
        self.chip_d = (1 - self.y) * 2 + 1 - self.x


def barrier(at):
    sem = pltpu.get_barrier_semaphore()
    for device in (at.to_x, at.to_y, at.to_c):
        pl.semaphore_signal(sem, inc=1, device_id=device, device_id_type=MESH)

    @pl.when(at.z < 3)
    def _():
        pl.semaphore_signal(sem, inc=1, device_id=at.up, device_id_type=MESH)

    @pl.when(at.z > 0)
    def _():
        pl.semaphore_signal(sem, inc=1, device_id=at.down, device_id_type=MESH)

    peers = 3 + (at.z < 3).astype(jnp.int32) + (at.z > 0).astype(jnp.int32)
    pl.semaphore_wait(sem, peers)


class Line:
    def __init__(self, at, buf, send, recv):
        self.at, self.buf, self.send, self.recv = at, buf, send, recv
        self.half = buf.shape[1] // 2

    def copy(self, block, half, way):
        part = self.buf.at[block, pl.ds(half * self.half, self.half)]
        return pltpu.make_async_remote_copy(
            src_ref=part, dst_ref=part,
            send_sem=self.send.at[way, block, half], recv_sem=self.recv.at[block, half],
            device_id=self.at.up if way == 0 else self.at.down, device_id_type=MESH)

    def start(self, half):
        at = self.at

        @pl.when(at.z < 3)
        def _():
            self.copy(at.z, half, 0).start()

        @pl.when(at.z > 0)
        def _():
            self.copy(at.z, half, 1).start()

    def step(self, s, half):
        at = self.at

        @pl.when(at.z - s >= 0)
        def _():
            self.copy(at.z - s, half, 0).wait_recv()

            @pl.when(at.z < 3)
            def _():
                self.copy(at.z - s, half, 0).start()

        @pl.when(at.z + s <= 3)
        def _():
            self.copy(at.z + s, half, 1).wait_recv()

            @pl.when(at.z > 0)
            def _():
                self.copy(at.z + s, half, 1).start()

    def finish(self, half):
        at = self.at
        for s in range(4):
            @pl.when((at.z - s >= 0) & (at.z < 3))
            def _():
                self.copy(at.z - s, half, 0).wait_send()

            @pl.when((at.z + s <= 3) & (at.z > 0))
            def _():
                self.copy(at.z + s, half, 1).wait_send()


class Plane:
    def __init__(self, at, buf, send, recv):
        self.at, self.buf, self.send, self.recv = at, buf, send, recv
        self.rows = buf.shape[0] // 8
        self.half = self.rows // 2
        self.sent = []

    def copy(self, chip, core, half, device, slot):
        start = pl.multiple_of((chip * 2 + core) * self.rows + half * self.half, 16)
        part = self.buf.at[pl.ds(start, self.half)]
        return pltpu.make_async_remote_copy(
            src_ref=part, dst_ref=part,
            send_sem=self.send.at[slot], recv_sem=self.recv.at[chip * 2 + core, half],
            device_id=device, device_id_type=MESH)

    def push(self, chip, half, device):
        one = self.copy(chip, self.at.c, half, device, len(self.sent))
        one.start()
        self.sent.append(one)

    def need(self, chip, core, half):
        self.copy(chip, core, half, self.at.to_c, 0).wait_recv()

    def start(self):
        at = self.at
        self.push(at.chip, 0, at.to_x)
        self.push(at.chip, 1, at.to_y)
        self.push(at.chip, 1, at.to_x)
        self.push(at.chip, 0, at.to_y)
        self.push(at.chip, 0, at.to_c)
        self.push(at.chip, 1, at.to_c)

    def first(self):
        at = self.at
        self.need(at.chip_x, at.c, 0)
        self.push(at.chip_x, 0, at.to_y)
        self.push(at.chip_x, 0, at.to_c)
        self.need(at.chip_y, at.c, 1)
        self.push(at.chip_y, 1, at.to_x)
        self.push(at.chip_y, 1, at.to_c)

    def second(self):
        at = self.at
        self.need(at.chip_x, at.c, 1)
        self.push(at.chip_x, 1, at.to_c)
        self.need(at.chip_y, at.c, 0)
        self.push(at.chip_y, 0, at.to_c)
        for half in range(2):
            self.need(at.chip, 1 - at.c, half)
            self.need(at.chip_x, 1 - at.c, half)
            self.need(at.chip_y, 1 - at.c, half)

    def third(self):
        at = self.at
        for half in range(2):
            self.need(at.chip_d, at.c, half)
            self.push(at.chip_d, half, at.to_c)
        for half in range(2):
            self.need(at.chip_d, 1 - at.c, half)

    def finish(self):
        for one in self.sent:
            one.wait_send()


SENDS = 14


def multiply(chunk, x_all, w_all, total):
    depth = x_all.shape[2]
    width = total.shape[1]
    rows = pl.ds(pl.multiple_of(chunk * depth, 32), depth)
    tiles = width // 256

    @pl.loop(0, tiles)
    def _(tile):
        cols = pl.ds(pl.multiple_of(tile * 256, 256), 256)
        total[:, cols] += jnp.dot(
            x_all[chunk], w_all[rows, cols], preferred_element_type=jnp.float32)

    if width % 256:
        rest = pl.ds(tiles * 256, width % 256)
        total[:, rest] += jnp.dot(
            x_all[chunk], w_all[rows, rest], preferred_element_type=jnp.float32)


def gather_multiply(at, line, plane, total):
    late = lambda j: (j == at.chip_d) | (j - at.z == 3) | (at.z - j == 3)
    line.start(0)
    plane.start()
    line.start(1)
    total[...] = jnp.zeros_like(total)
    line.step(1, 0)
    plane.first()
    line.step(1, 1)
    line.step(2, 0)
    line.step(2, 1)
    plane.second()

    @pl.loop(0, 4)
    def _(j):
        @pl.when(jnp.logical_not(late(j)))
        def _():
            multiply(j, line.buf, plane.buf, total)

    line.step(3, 0)
    line.step(3, 1)
    plane.third()

    @pl.loop(0, 4)
    def _(j):
        @pl.when(late(j))
        def _():
            multiply(j, line.buf, plane.buf, total)


def finish(line, plane):
    line.finish(0)
    line.finish(1)
    plane.finish()


def project_kernel(x, wq, wk, wv, gains, cosine, sine, q, k, v,
                   x_all, w_all, total, zs, zr, ps, pr, local):
    at = Place()
    shard = w_all.shape[0] // 8
    nq, nk = wq.shape[1], wk.shape[1]
    mine = pl.ds(pl.multiple_of((at.chip * 2 + at.c) * shard, 16), shard)
    loads = [
        pltpu.make_async_copy(x, x_all.at[at.z], local.at[0]),
        pltpu.make_async_copy(wq, w_all.at[mine, pl.ds(0, nq)], local.at[1]),
        pltpu.make_async_copy(wk, w_all.at[mine, pl.ds(nq, nk)], local.at[2]),
        pltpu.make_async_copy(wv, w_all.at[mine, pl.ds(nq + nk, nk)], local.at[3]),
    ]
    for load in loads:
        load.start()
    barrier(at)
    for load in loads:
        load.wait()
    line, plane = Line(at, x_all, zs, zr), Plane(at, w_all, ps, pr)
    gather_multiply(at, line, plane, total)

    def head(col, gain):
        block = total[:, pl.ds(pl.multiple_of(col, 128), 128)]
        mean_square = jnp.mean(block * block, axis=-1, keepdims=True)
        normed = block * lax.rsqrt(mean_square + 1e-06) * gain
        turned = normed * cosine[...] + pltpu.roll(normed, 64, 1) * sine[...]
        return turned.astype(jnp.bfloat16)

    @pl.loop(0, nq // 128)
    def _(h):
        q[:, pl.ds(pl.multiple_of(h * 128, 128), 128)] = head(h * 128, gains[0:1, :])

    @pl.loop(0, nk // 128)
    def _(h):
        k[:, pl.ds(pl.multiple_of(h * 128, 128), 128)] = head(nq + h * 128, gains[1:2, :])

    v[...] = total[:, nq + nk:].astype(jnp.bfloat16)
    finish(line, plane)


def output_kernel(x, w, out, x_all, w_all, total, zs, zr, ps, pr, local):
    at = Place()
    shard = w_all.shape[0] // 8
    mine = pl.ds(pl.multiple_of((at.chip * 2 + at.c) * shard, 16), shard)
    loads = [
        pltpu.make_async_copy(x, x_all.at[at.z], local.at[0]),
        pltpu.make_async_copy(w, w_all.at[mine], local.at[1]),
    ]
    for load in loads:
        load.start()
    barrier(at)
    for load in loads:
        load.wait()
    line, plane = Line(at, x_all, zs, zr), Plane(at, w_all, ps, pr)
    gather_multiply(at, line, plane, total)
    out[...] = total[...].astype(jnp.bfloat16)
    finish(line, plane)


def gather_scratch(rows, depth, width):
    return [
        pltpu.VMEM((4, rows, depth), jnp.bfloat16),
        pltpu.VMEM((4 * depth, width), jnp.bfloat16),
        pltpu.VMEM((rows, width), jnp.float32),
        pltpu.SemaphoreType.DMA((2, 4, 2)),
        pltpu.SemaphoreType.DMA((4, 2)),
        pltpu.SemaphoreType.DMA((SENDS,)),
        pltpu.SemaphoreType.DMA((8, 2)),
        pltpu.SemaphoreType.DMA((4,)),
    ]


HBM = pl.BlockSpec(memory_space=pl.ANY)
LOCAL = pl.BlockSpec(memory_space=pltpu.VMEM)


def angles_of(positions):
    freqs = 10000.0 ** (-(jnp.arange(64, dtype=jnp.float32) * 2.0 / HEAD_SIZE))
    angles = positions.astype(jnp.float32)[:, None] * freqs[None, :]
    cosine, sine = jnp.cos(angles), jnp.sin(angles)
    return jnp.concatenate([cosine, cosine], 1), jnp.concatenate([-sine, sine], 1)


def fused(tokens, w_query, key_weight, value_weight, w_output, query_gain, key_gain):
    rows, depth = tokens.shape
    nq, nk = w_query.shape[1], key_weight.shape[1]
    base = lax.axis_index(("seq", "row")) * rows
    positions = base + jnp.arange(rows, dtype=jnp.int32)
    cosine, sine = angles_of(positions)
    gains = jnp.stack([query_gain, key_gain])
    bf16 = jnp.bfloat16
    queries, key_flat, value_flat = pl.pallas_call(
        project_kernel,
        out_shape=[jax.ShapeDtypeStruct((rows, n), bf16) for n in (nq, nk, nk)],
        in_specs=[HBM] * 4 + [LOCAL] * 3,
        out_specs=[LOCAL] * 3,
        scratch_shapes=gather_scratch(rows, depth, nq + 2 * nk),
        compiler_params=pltpu.CompilerParams(
            collective_id=0, has_side_effects=True, vmem_limit_bytes=56 * MIB),
    )(tokens, w_query, key_weight, value_weight, gains, cosine, sine)
    kv_heads = nk // HEAD_SIZE
    one = shifted((key_flat, value_flat), ("seq", "row"), 1)
    two = shifted((key_flat, value_flat), ("seq", "row"), 2)
    key_rows = jnp.concatenate([two[0], one[0], key_flat], 0)
    value_rows = jnp.concatenate([two[1], one[1], value_flat], 0)
    kpos = base - 2 * rows + jnp.arange(3 * rows, dtype=jnp.int32)
    mixed = attend(
        queries.reshape(rows, nq // HEAD_SIZE, HEAD_SIZE),
        key_rows.reshape(3 * rows, kv_heads, HEAD_SIZE),
        value_rows.reshape(3 * rows, kv_heads, HEAD_SIZE), positions, kpos)
    return pl.pallas_call(
        output_kernel,
        out_shape=jax.ShapeDtypeStruct((rows, w_output.shape[1]), bf16),
        in_specs=[HBM] * 2,
        out_specs=LOCAL,
        scratch_shapes=gather_scratch(rows, nq, w_output.shape[1]),
        compiler_params=pltpu.CompilerParams(
            collective_id=1, has_side_effects=True, vmem_limit_bytes=48 * MIB),
    )(mixed, w_output)


def solution(mesh):
    small = dict(mesh.shape) == {"seq": 2, "row": 4, "col": 4}
    split = P(("seq", "row"), "col")
    return jax.shard_map(
        fused if small else shards,
        mesh=mesh,
        in_specs=(split, split, split, split, split, P(), P()),
        out_specs=split,
        check_vma=False,
    )
```

```python
import jax
import jax.numpy as jnp
from jax import lax
from jax.experimental import pallas as pl
from jax.experimental.pallas import tpu as pltpu
from jax.sharding import PartitionSpec as P

HEAD_SIZE = 128
WINDOW_KEYS = 1024


query_scale = 168.0 ** (-0.5)


def shifted(block, axis, distance):
    devices = range(lax.axis_size(axis))
    route = [(i - distance, i) for i in devices if i - distance in devices]
    return lax.ppermute(block, axis, route)


def head_norm(block, gain):
    mean_square = jnp.mean(block * block, axis=-1, keepdims=True)
    return block * lax.rsqrt(mean_square + 1e-06) * gain


def rotate(block, positions):
    half = block.shape[-1] // 2
    freqs = 10000.0 ** (-(jnp.arange(half, dtype=jnp.float32) * 2.0 / block.shape[-1]))
    angles = positions.astype(jnp.float32)[:, None] * freqs[None, :]
    cosine = jnp.cos(angles)[:, None, :]
    sine = jnp.sin(angles)[:, None, :]
    first = block[..., :half]
    second = block[..., half:]
    return jnp.concatenate(
        [first * cosine - second * sine, second * cosine + first * sine], axis=-1
    )


def attend(queries, key_states, value_states, qpos, kpos):
    rows = queries.shape[0]
    kv_heads = key_states.shape[1]
    grouped = queries.reshape(rows, kv_heads, 2, HEAD_SIZE)
    scores = (
        jnp.einsum("bhgd,khd->hgbk", grouped, key_states, preferred_element_type=jnp.float32)
        * query_scale
    )
    gap = qpos[:, None] - kpos[None, :]
    valid = (kpos[None, :] >= 0) & (gap >= 0) & (gap < WINDOW_KEYS)
    scores = jnp.where(valid[None, None], scores, -1e30)
    top = jnp.max(scores, axis=-1, keepdims=True)
    weights = jnp.exp(scores - top)
    weights = (weights / jnp.sum(weights, axis=-1, keepdims=True)).astype(jnp.bfloat16)
    mixed = jnp.einsum("hgbk,khd->bhgd", weights, value_states, preferred_element_type=jnp.float32)
    return mixed.astype(jnp.bfloat16).reshape(rows, kv_heads * 2 * HEAD_SIZE)


def shards(tokens, w_query, key_weight, value_weight, w_output, query_gain, key_gain):
    rows = tokens.shape[0]
    whole = lax.all_gather(tokens, "col", axis=1, tiled=True)
    columns = whole
    proj_q = jnp.dot(
        columns,
        lax.all_gather(w_query, ("seq", "row"), axis=0, tiled=True),
        preferred_element_type=jnp.float32,
    )
    projected_key = jnp.dot(
        columns,
        lax.all_gather(key_weight, ("seq", "row"), axis=0, tiled=True),
        preferred_element_type=jnp.float32,
    )
    proj_v = jnp.dot(
        columns,
        lax.all_gather(value_weight, ("seq", "row"), axis=0, tiled=True),
        preferred_element_type=jnp.float32,
    )
    base = lax.axis_index(("seq", "row")) * rows
    positions = base + jnp.arange(rows, dtype=jnp.int32)
    q_heads = proj_q.shape[1] // HEAD_SIZE
    kv_heads = projected_key.shape[1] // HEAD_SIZE
    queries = rotate(
        head_norm(proj_q.reshape(rows, q_heads, HEAD_SIZE), query_gain), positions
    ).astype(jnp.bfloat16)
    key_states = rotate(
        head_norm(projected_key.reshape(rows, kv_heads, HEAD_SIZE), key_gain), positions
    ).astype(jnp.bfloat16)
    key_flat = key_states.reshape(rows, kv_heads * HEAD_SIZE)
    value_flat = proj_v.astype(jnp.bfloat16)
    prior_one = shifted((key_flat, value_flat), ("seq", "row"), 1)
    prior_two = shifted((key_flat, value_flat), ("seq", "row"), 2)
    key_rows = jnp.concatenate([prior_two[0], prior_one[0], key_flat], axis=0).reshape(
        3 * rows, kv_heads, HEAD_SIZE
    )
    value_rows = jnp.concatenate([prior_two[1], prior_one[1], value_flat], axis=0).reshape(
        3 * rows, kv_heads, HEAD_SIZE
    )
    kpos = base - 2 * rows + jnp.arange(3 * rows, dtype=jnp.int32)
    mixed = attend(queries, key_rows, value_rows, positions, kpos)
    all_heads = lax.all_gather(mixed, "col", axis=1, tiled=True)
    columns = all_heads
    attended = jnp.dot(
        columns,
        lax.all_gather(w_output, ("seq", "row"), axis=0, tiled=True),
        preferred_element_type=jnp.float32,
    )
    return attended.astype(jnp.bfloat16)


MESH = pl.DeviceIdType.MESH
MIB = 1 << 20
SENDS = 14
LOG2_E = 1.4426950408889634


class Place:
    def __init__(self):
        self.y = lax.axis_index("seq")
        row = lax.axis_index("row")
        self.x, self.c = row // 2, row % 2
        self.z = lax.axis_index("col")
        self.to_x = {"seq": self.y, "row": (1 - self.x) * 2 + self.c, "col": self.z}
        self.to_y = {"seq": 1 - self.y, "row": row, "col": self.z}
        self.to_c = {"seq": self.y, "row": self.x * 2 + 1 - self.c, "col": self.z}
        self.up = {"seq": self.y, "row": row, "col": self.z + 1}
        self.down = {"seq": self.y, "row": row, "col": self.z - 1}
        self.to_d = {"seq": 1 - self.y, "row": (1 - self.x) * 2 + self.c, "col": self.z}
        self.chip = self.y * 2 + self.x
        after = (self.chip + 1) % 4
        self.after = {"seq": after // 2, "row": (after % 2) * 2 + self.c, "col": self.z}
        self.chip_x = self.y * 2 + 1 - self.x
        self.chip_y = (1 - self.y) * 2 + self.x
        self.chip_d = (1 - self.y) * 2 + 1 - self.x


def barrier(at):
    sem = pltpu.get_barrier_semaphore()
    for device in (at.to_x, at.to_y, at.to_c, at.to_d):
        pl.semaphore_signal(sem, inc=1, device_id=device, device_id_type=MESH)

    @pl.when(at.z < 3)
    def _():
        pl.semaphore_signal(sem, inc=1, device_id=at.up, device_id_type=MESH)

    @pl.when(at.z > 0)
    def _():
        pl.semaphore_signal(sem, inc=1, device_id=at.down, device_id_type=MESH)

    peers = 4 + (at.z < 3).astype(jnp.int32) + (at.z > 0).astype(jnp.int32)
    pl.semaphore_wait(sem, peers)


class Line:
    def __init__(self, at, part, send, recv):
        self.at, self.part, self.send, self.recv = at, part, send, recv

    def copy(self, block, part, way):
        piece = self.part(block, part)
        return pltpu.make_async_remote_copy(
            src_ref=piece, dst_ref=piece,
            send_sem=self.send.at[way, block, part], recv_sem=self.recv.at[block, part],
            device_id=self.at.up if way == 0 else self.at.down, device_id_type=MESH)

    def start(self, part):
        at = self.at

        @pl.when(at.z < 3)
        def _():
            self.copy(at.z, part, 0).start()

        @pl.when(at.z > 0)
        def _():
            self.copy(at.z, part, 1).start()

    def step(self, s, part):
        at = self.at

        @pl.when(at.z - s >= 0)
        def _():
            self.copy(at.z - s, part, 0).wait_recv()

            @pl.when(at.z < 3)
            def _():
                self.copy(at.z - s, part, 0).start()

        @pl.when(at.z + s <= 3)
        def _():
            self.copy(at.z + s, part, 1).wait_recv()

            @pl.when(at.z > 0)
            def _():
                self.copy(at.z + s, part, 1).start()

    def finish(self, parts):
        at = self.at
        for s in range(4):
            for part in range(parts):
                @pl.when((at.z - s >= 0) & (at.z < 3))
                def _():
                    self.copy(at.z - s, part, 0).wait_send()

                @pl.when((at.z + s <= 3) & (at.z > 0))
                def _():
                    self.copy(at.z + s, part, 1).wait_send()


class Plane:
    def __init__(self, at, buf, send, recv):
        self.at, self.buf, self.send, self.recv = at, buf, send, recv
        self.rows = buf.shape[0] // 8
        self.half = self.rows // 2
        self.sent = []

    def copy(self, chip, core, half, device, slot):
        start = pl.multiple_of((chip * 2 + core) * self.rows + half * self.half, 16)
        part = self.buf.at[pl.ds(start, self.half)]
        return pltpu.make_async_remote_copy(
            src_ref=part, dst_ref=part,
            send_sem=self.send.at[slot], recv_sem=self.recv.at[chip * 2 + core, half],
            device_id=device, device_id_type=MESH)

    def push(self, chip, half, device):
        one = self.copy(chip, self.at.c, half, device, len(self.sent))
        one.start()
        self.sent.append(one)

    def need(self, chip, core, half):
        self.copy(chip, core, half, self.at.to_c, 0).wait_recv()

    def start(self):
        at = self.at
        self.push(at.chip, 0, at.to_x)
        self.push(at.chip, 1, at.to_y)
        self.push(at.chip, 1, at.to_x)
        self.push(at.chip, 0, at.to_y)
        self.push(at.chip, 0, at.to_c)
        self.push(at.chip, 1, at.to_c)

    def first(self):
        at = self.at
        self.need(at.chip_x, at.c, 0)
        self.push(at.chip_x, 0, at.to_y)
        self.push(at.chip_x, 0, at.to_c)
        self.need(at.chip_y, at.c, 1)
        self.push(at.chip_y, 1, at.to_x)
        self.push(at.chip_y, 1, at.to_c)

    def second(self):
        at = self.at
        self.need(at.chip_x, at.c, 1)
        self.push(at.chip_x, 1, at.to_c)
        self.need(at.chip_y, at.c, 0)
        self.push(at.chip_y, 0, at.to_c)
        for half in range(2):
            self.need(at.chip, 1 - at.c, half)
            self.need(at.chip_x, 1 - at.c, half)
            self.need(at.chip_y, 1 - at.c, half)

    def third(self):
        at = self.at
        for half in range(2):
            self.need(at.chip_d, at.c, half)
            self.push(at.chip_d, half, at.to_c)
        for half in range(2):
            self.need(at.chip_d, 1 - at.c, half)

    def finish(self):
        for one in self.sent:
            one.wait_send()


class Halo:
    def __init__(self, at, kv, rows, sems):
        self.at, self.kv, self.rows, self.sems = at, kv, rows, sems

    def piece(self, block, h):
        cols = pl.ds(pl.multiple_of(h * 256, 256), 256)
        return self.kv.at[pl.ds(block * self.rows, self.rows), cols]

    def on(self, h):
        return pltpu.make_async_remote_copy(
            src_ref=self.piece(2, h), dst_ref=self.piece(0, h),
            send_sem=self.sems.at[0, h], recv_sem=self.sems.at[1, h],
            device_id=self.at.after, device_id_type=MESH)

    def across(self, block, h):
        return pltpu.make_async_remote_copy(
            src_ref=self.piece(block, h), dst_ref=self.piece(1, h),
            send_sem=self.sems.at[2, h], recv_sem=self.sems.at[3, h],
            device_id=self.at.to_c, device_id_type=MESH)

    def start(self, h):
        @pl.when(self.at.chip < 3)
        def _():
            self.on(h).start()

        @pl.when(self.at.c == 0)
        def _():
            self.across(2, h).start()

    def need(self, h):
        at = self.at

        @pl.when(at.chip > 0)
        def _():
            self.on(h).wait_recv()

            @pl.when(at.c == 1)
            def _():
                self.across(0, h).start()

        @pl.when((at.chip > 0) | (at.c == 1))
        def _():
            self.across(0, h).wait_recv()

    def finish(self, h):
        at = self.at

        @pl.when(at.chip < 3)
        def _():
            self.on(h).wait_send()

        @pl.when((at.chip > 0) | (at.c == 0))
        def _():
            self.across(0, h).wait_send()


def multiply(chunk, x_all, w_all, total, low, high):
    depth = x_all.shape[2]
    rows = pl.ds(pl.multiple_of(chunk * depth, 32), depth)
    tiles = (high - low) // 256

    @pl.loop(0, tiles)
    def _(tile):
        cols = pl.ds(pl.multiple_of(low + tile * 256, 256), 256)
        total[:, cols] += jnp.dot(
            x_all[chunk], w_all[rows, cols], preferred_element_type=jnp.float32)

    if (high - low) % 256:
        rest = pl.ds(low + tiles * 256, (high - low) % 256)
        total[:, rest] += jnp.dot(
            x_all[chunk], w_all[rows, rest], preferred_element_type=jnp.float32)


def kernel(x, wq, wk, wv, wo, gains, cosine, sine, out,
           x_all, w_all, total, o_all, mixed, kv, q,
           zs, zr, ps, pr, ms, mr, os, orr, hs, local):
    at = Place()
    rows = x.shape[0]
    nq, nk = wq.shape[1], wk.shape[1]
    features = wo.shape[1]
    heads = nk // 128
    shard, shard_o = w_all.shape[0] // 8, o_all.shape[0] // 8
    device = at.chip * 2 + at.c
    mine = pl.ds(pl.multiple_of(device * shard, 16), shard)
    mine_o = pl.ds(pl.multiple_of(device * shard_o, 16), shard_o)
    loads = [
        pltpu.make_async_copy(x, x_all.at[at.z], local.at[0]),
        pltpu.make_async_copy(wq, w_all.at[mine, pl.ds(0, nq)], local.at[1]),
        pltpu.make_async_copy(wk, w_all.at[mine, pl.ds(nq, nk)], local.at[2]),
        pltpu.make_async_copy(wv, w_all.at[mine, pl.ds(nq + nk, nk)], local.at[3]),
    ]
    load_o = pltpu.make_async_copy(wo, o_all.at[mine_o], local.at[4])
    for load in loads:
        load.start()
    barrier(at)
    for load in loads:
        load.wait()
    load_o.start()
    half = rows // 2
    line = Line(at, lambda b, p: x_all.at[b, pl.ds(p * half, half)], zs, zr)
    line_m = Line(at, lambda b, p: mixed.at[b, :, pl.ds(p * 256, 256)], ms, mr)
    plane, plane_o = Plane(at, w_all, ps, pr), Plane(at, o_all, os, orr)
    halo = Halo(at, kv, rows, hs)

    def late(j):
        return (j == at.chip_d) | (j - at.z == 3) | (at.z - j == 3)

    line.start(0)
    plane.start()
    line.start(1)
    total[...] = jnp.zeros_like(total)

    @pl.when(at.chip == 0)
    def _():
        kv[pl.ds(0, rows), :] = jnp.zeros((rows, 2 * nk), jnp.bfloat16)

        @pl.when(at.c == 0)
        def _():
            kv[pl.ds(rows, rows), :] = jnp.zeros((rows, 2 * nk), jnp.bfloat16)

    line.step(1, 0)
    plane.first()
    line.step(1, 1)
    line.step(2, 0)
    line.step(2, 1)
    plane.second()

    @pl.loop(0, 4)
    def _(j):
        @pl.when(jnp.logical_not(late(j)))
        def _():
            multiply(j, x_all, w_all, total, 0, nq + 2 * nk)

    line.step(3, 0)
    line.step(3, 1)
    plane.third()

    def late_columns(low, high):
        @pl.loop(0, 4)
        def _(j):
            @pl.when(late(j))
            def _():
                multiply(j, x_all, w_all, total, low, high)

    def head(col, gain):
        block = total[:, pl.ds(pl.multiple_of(col, 128), 128)]
        mean_square = jnp.mean(block * block, axis=-1, keepdims=True)
        normed = block * lax.rsqrt(mean_square + 1e-06) * gain
        turned = normed * cosine[...] + pltpu.roll(normed, 64, 1) * sine[...]
        return turned.astype(jnp.bfloat16)

    late_columns(nq, nq + 2 * nk)
    own = pl.ds(2 * rows, rows)

    @pl.loop(0, heads)
    def _(h):
        kv[own, pl.ds(pl.multiple_of(h * 256, 256), 128)] = head(nq + h * 128, gains[1:2, :])
        values = total[:, pl.ds(pl.multiple_of(nq + nk + h * 128, 128), 128)]
        kv[own, pl.ds(pl.multiple_of(h * 256 + 128, 128), 128)] = values.astype(jnp.bfloat16)
        halo.start(h)

    late_columns(0, nq)

    @pl.loop(0, nq // 128)
    def _(h):
        q[:, pl.ds(pl.multiple_of(h * 128, 128), 128)] = head(h * 128, gains[0:1, :])

    span = half + 2 * rows
    for tile in range(2):
        query = lax.broadcasted_iota(jnp.int32, (half, span), 0)
        key = lax.broadcasted_iota(jnp.int32, (half, span), 1)
        low = 2 * rows - device * rows - tile * half
        valid = (key > query) & (key <= query + WINDOW_KEYS) & (key >= low)
        total[pl.ds(tile * half, half), 0:span] = jnp.where(valid, 0.0, -1e30)

    def attend_head(h):
        @pl.loop(0, 2)
        def _(tile):
            first = pl.multiple_of(tile * half, half)
            keys = kv[pl.ds(first, span), h * 256:h * 256 + 128]
            values = kv[pl.ds(first, span), h * 256 + 128:h * 256 + 256]
            for g in range(2):
                cols = slice((2 * h + g) * 128, (2 * h + g + 1) * 128)
                scores = lax.dot_general(
                    q[pl.ds(first, half), cols], keys, (((1,), (1,)), ((), ())),
                    preferred_element_type=jnp.float32)
                scores = scores + total[pl.ds(first, half), 0:span]
                top = jnp.max(scores, axis=-1, keepdims=True)
                weights = jnp.exp2((scores - top) * (query_scale * LOG2_E))
                inverse = 1.0 / jnp.sum(weights, axis=-1, keepdims=True)
                weights = (weights * inverse).astype(jnp.bfloat16)
                mixed[at.z, pl.ds(first, half), cols] = jnp.dot(
                    weights, values, preferred_element_type=jnp.float32).astype(jnp.bfloat16)

    for h in range(heads):
        halo.need(h)
        if h == heads - 1:
            load_o.wait()
            plane_o.start()
        attend_head(h)
        line_m.start(h)
        if h > 0:
            line_m.step(1, h - 1)

    total[:, 0:features] = jnp.zeros((rows, features), jnp.float32)
    line_m.step(1, heads - 1)
    line_m.step(2, 0)
    plane_o.first()
    line_m.step(2, 1)
    line_m.step(2, 2)
    plane_o.second()
    line_m.step(2, 3)
    plane_o.third()

    def near(j):
        return (j - at.z < 3) & (at.z - j < 3)

    @pl.loop(0, 4)
    def _(j):
        @pl.when(near(j))
        def _():
            multiply(j, mixed, o_all, total, 0, features)

    for part in range(heads):
        line_m.step(3, part)

    @pl.loop(0, 4)
    def _(j):
        @pl.when(jnp.logical_not(near(j)))
        def _():
            multiply(j, mixed, o_all, total, 0, features)

    out[...] = total[:, 0:features].astype(jnp.bfloat16)
    line.finish(2)
    line_m.finish(heads)
    plane.finish()
    plane_o.finish()
    for h in range(heads):
        halo.finish(h)


def angles_of(positions):
    freqs = 10000.0 ** (-(jnp.arange(64, dtype=jnp.float32) * 2.0 / HEAD_SIZE))
    angles = positions.astype(jnp.float32)[:, None] * freqs[None, :]
    cosine, sine = jnp.cos(angles), jnp.sin(angles)
    return jnp.concatenate([cosine, cosine], 1), jnp.concatenate([-sine, sine], 1)


def fused(tokens, w_query, key_weight, value_weight, w_output, query_gain, key_gain):
    rows, depth = tokens.shape
    nq, nk = w_query.shape[1], key_weight.shape[1]
    features = w_output.shape[1]
    base = lax.axis_index(("seq", "row")) * rows
    cosine, sine = angles_of(base + jnp.arange(rows, dtype=jnp.int32))
    gains = jnp.stack([query_gain, key_gain])
    hbm = pl.BlockSpec(memory_space=pl.ANY)
    vmem = pl.BlockSpec(memory_space=pltpu.VMEM)
    bf16, dma = jnp.bfloat16, pltpu.SemaphoreType.DMA
    return pl.pallas_call(
        kernel,
        out_shape=jax.ShapeDtypeStruct((rows, features), bf16),
        in_specs=[hbm] * 5 + [vmem] * 3,
        out_specs=vmem,
        scratch_shapes=[
            pltpu.VMEM((4, rows, depth), bf16),
            pltpu.VMEM((4 * depth, nq + 2 * nk), bf16),
            pltpu.VMEM((rows, nq + 2 * nk), jnp.float32),
            pltpu.VMEM((4 * nq, features), bf16),
            pltpu.VMEM((4, rows, nq), bf16),
            pltpu.VMEM((3 * rows, 2 * nk), bf16),
            pltpu.VMEM((rows, nq), bf16),
            dma((2, 4, 2)), dma((4, 2)), dma((SENDS,)), dma((8, 2)),
            dma((2, 4, 4)), dma((4, 4)), dma((SENDS,)), dma((8, 2)),
            dma((4, 4)), dma((5,)),
        ],
        compiler_params=pltpu.CompilerParams(
            collective_id=0, has_side_effects=True, vmem_limit_bytes=62 * MIB),
    )(tokens, w_query, key_weight, value_weight, w_output, gains, cosine, sine)


def solution(mesh):
    small = dict(mesh.shape) == {"seq": 2, "row": 4, "col": 4}
    split = P(("seq", "row"), "col")
    return jax.shard_map(
        fused if small else shards,
        mesh=mesh,
        in_specs=(split, split, split, split, split, P(), P()),
        out_specs=split,
        check_vma=False,
    )
```

```python
import jax
import jax.numpy as jnp
from jax import lax
from jax.experimental import pallas as pl
from jax.experimental.pallas import tpu as pltpu
from jax.sharding import PartitionSpec as P

HEAD_SIZE = 128
WINDOW_KEYS = 1024


query_scale = 168.0 ** (-0.5)


def shifted(block, axis, distance):
    devices = range(lax.axis_size(axis))
    route = [(i - distance, i) for i in devices if i - distance in devices]
    return lax.ppermute(block, axis, route)


def head_norm(block, gain):
    mean_square = jnp.mean(block * block, axis=-1, keepdims=True)
    return block * lax.rsqrt(mean_square + 1e-06) * gain


def rotate(block, positions):
    half = block.shape[-1] // 2
    freqs = 10000.0 ** (-(jnp.arange(half, dtype=jnp.float32) * 2.0 / block.shape[-1]))
    angles = positions.astype(jnp.float32)[:, None] * freqs[None, :]
    cosine = jnp.cos(angles)[:, None, :]
    sine = jnp.sin(angles)[:, None, :]
    first = block[..., :half]
    second = block[..., half:]
    return jnp.concatenate(
        [first * cosine - second * sine, second * cosine + first * sine], axis=-1
    )


def attend(queries, key_states, value_states, qpos, kpos):
    rows = queries.shape[0]
    kv_heads = key_states.shape[1]
    grouped = queries.reshape(rows, kv_heads, 2, HEAD_SIZE)
    scores = (
        jnp.einsum("bhgd,khd->hgbk", grouped, key_states, preferred_element_type=jnp.float32)
        * query_scale
    )
    gap = qpos[:, None] - kpos[None, :]
    valid = (kpos[None, :] >= 0) & (gap >= 0) & (gap < WINDOW_KEYS)
    scores = jnp.where(valid[None, None], scores, -1e30)
    top = jnp.max(scores, axis=-1, keepdims=True)
    weights = jnp.exp(scores - top)
    weights = (weights / jnp.sum(weights, axis=-1, keepdims=True)).astype(jnp.bfloat16)
    mixed = jnp.einsum("hgbk,khd->bhgd", weights, value_states, preferred_element_type=jnp.float32)
    return mixed.astype(jnp.bfloat16).reshape(rows, kv_heads * 2 * HEAD_SIZE)


def shards(tokens, w_query, key_weight, value_weight, w_output, query_gain, key_gain):
    rows = tokens.shape[0]
    whole = lax.all_gather(tokens, "col", axis=1, tiled=True)
    columns = whole
    proj_q = jnp.dot(
        columns,
        lax.all_gather(w_query, ("seq", "row"), axis=0, tiled=True),
        preferred_element_type=jnp.float32,
    )
    projected_key = jnp.dot(
        columns,
        lax.all_gather(key_weight, ("seq", "row"), axis=0, tiled=True),
        preferred_element_type=jnp.float32,
    )
    proj_v = jnp.dot(
        columns,
        lax.all_gather(value_weight, ("seq", "row"), axis=0, tiled=True),
        preferred_element_type=jnp.float32,
    )
    base = lax.axis_index(("seq", "row")) * rows
    positions = base + jnp.arange(rows, dtype=jnp.int32)
    q_heads = proj_q.shape[1] // HEAD_SIZE
    kv_heads = projected_key.shape[1] // HEAD_SIZE
    queries = rotate(
        head_norm(proj_q.reshape(rows, q_heads, HEAD_SIZE), query_gain), positions
    ).astype(jnp.bfloat16)
    key_states = rotate(
        head_norm(projected_key.reshape(rows, kv_heads, HEAD_SIZE), key_gain), positions
    ).astype(jnp.bfloat16)
    key_flat = key_states.reshape(rows, kv_heads * HEAD_SIZE)
    value_flat = proj_v.astype(jnp.bfloat16)
    prior_one = shifted((key_flat, value_flat), ("seq", "row"), 1)
    prior_two = shifted((key_flat, value_flat), ("seq", "row"), 2)
    key_rows = jnp.concatenate([prior_two[0], prior_one[0], key_flat], axis=0).reshape(
        3 * rows, kv_heads, HEAD_SIZE
    )
    value_rows = jnp.concatenate([prior_two[1], prior_one[1], value_flat], axis=0).reshape(
        3 * rows, kv_heads, HEAD_SIZE
    )
    kpos = base - 2 * rows + jnp.arange(3 * rows, dtype=jnp.int32)
    mixed = attend(queries, key_rows, value_rows, positions, kpos)
    all_heads = lax.all_gather(mixed, "col", axis=1, tiled=True)
    columns = all_heads
    attended = jnp.dot(
        columns,
        lax.all_gather(w_output, ("seq", "row"), axis=0, tiled=True),
        preferred_element_type=jnp.float32,
    )
    return attended.astype(jnp.bfloat16)


MESH = pl.DeviceIdType.MESH
MIB = 1 << 20
SENDS = 14
LOG2_E = 1.4426950408889634


class Place:
    def __init__(self):
        self.y = lax.axis_index("seq")
        row = lax.axis_index("row")
        self.x, self.c = row // 2, row % 2
        self.z = lax.axis_index("col")
        self.to_x = {"seq": self.y, "row": (1 - self.x) * 2 + self.c, "col": self.z}
        self.to_y = {"seq": 1 - self.y, "row": row, "col": self.z}
        self.to_c = {"seq": self.y, "row": self.x * 2 + 1 - self.c, "col": self.z}
        self.up = {"seq": self.y, "row": row, "col": self.z + 1}
        self.down = {"seq": self.y, "row": row, "col": self.z - 1}
        self.to_d = {"seq": 1 - self.y, "row": (1 - self.x) * 2 + self.c, "col": self.z}
        self.chip = self.y * 2 + self.x
        after = (self.chip + 1) % 4
        self.after = {"seq": after // 2, "row": (after % 2) * 2 + self.c, "col": self.z}
        self.chip_x = self.y * 2 + 1 - self.x
        self.chip_y = (1 - self.y) * 2 + self.x
        self.chip_d = (1 - self.y) * 2 + 1 - self.x


def barrier(at):
    sem = pltpu.get_barrier_semaphore()
    for device in (at.to_x, at.to_y, at.to_c, at.to_d):
        pl.semaphore_signal(sem, inc=1, device_id=device, device_id_type=MESH)

    @pl.when(at.z < 3)
    def _():
        pl.semaphore_signal(sem, inc=1, device_id=at.up, device_id_type=MESH)

    @pl.when(at.z > 0)
    def _():
        pl.semaphore_signal(sem, inc=1, device_id=at.down, device_id_type=MESH)

    peers = 4 + (at.z < 3).astype(jnp.int32) + (at.z > 0).astype(jnp.int32)
    pl.semaphore_wait(sem, peers)


class Line:
    def __init__(self, at, part, send, recv):
        self.at, self.part, self.send, self.recv = at, part, send, recv

    def copy(self, block, part, way):
        piece = self.part(block, part)
        return pltpu.make_async_remote_copy(
            src_ref=piece, dst_ref=piece,
            send_sem=self.send.at[way, block, part], recv_sem=self.recv.at[block, part],
            device_id=self.at.up if way == 0 else self.at.down, device_id_type=MESH)

    def start(self, part):
        at = self.at

        @pl.when(at.z < 3)
        def _():
            self.copy(at.z, part, 0).start()

        @pl.when(at.z > 0)
        def _():
            self.copy(at.z, part, 1).start()

    def step(self, s, part):
        at = self.at

        @pl.when(at.z - s >= 0)
        def _():
            self.copy(at.z - s, part, 0).wait_recv()

            @pl.when(at.z < 3)
            def _():
                self.copy(at.z - s, part, 0).start()

        @pl.when(at.z + s <= 3)
        def _():
            self.copy(at.z + s, part, 1).wait_recv()

            @pl.when(at.z > 0)
            def _():
                self.copy(at.z + s, part, 1).start()

    def finish(self, parts):
        at = self.at
        for s in range(4):
            for part in range(parts):
                @pl.when((at.z - s >= 0) & (at.z < 3))
                def _():
                    self.copy(at.z - s, part, 0).wait_send()

                @pl.when((at.z + s <= 3) & (at.z > 0))
                def _():
                    self.copy(at.z + s, part, 1).wait_send()


class Plane:
    def __init__(self, at, part, send, recv):
        self.at, self.part, self.send, self.recv = at, part, send, recv
        self.sent = []

    def copy(self, chip, core, half, device, slot):
        piece = self.part(chip * 2 + core, half)
        return pltpu.make_async_remote_copy(
            src_ref=piece, dst_ref=piece,
            send_sem=self.send.at[slot], recv_sem=self.recv.at[chip * 2 + core, half],
            device_id=device, device_id_type=MESH)

    def push(self, chip, half, device):
        one = self.copy(chip, self.at.c, half, device, len(self.sent))
        one.start()
        self.sent.append(one)

    def need(self, chip, core, half):
        self.copy(chip, core, half, self.at.to_c, 0).wait_recv()

    def start(self):
        at = self.at
        self.push(at.chip, 0, at.to_x)
        self.push(at.chip, 1, at.to_y)
        self.push(at.chip, 1, at.to_x)
        self.push(at.chip, 0, at.to_y)
        self.push(at.chip, 0, at.to_c)
        self.push(at.chip, 1, at.to_c)

    def first(self):
        at = self.at
        self.need(at.chip_x, at.c, 0)
        self.push(at.chip_x, 0, at.to_y)
        self.push(at.chip_x, 0, at.to_c)
        self.need(at.chip_y, at.c, 1)
        self.push(at.chip_y, 1, at.to_x)
        self.push(at.chip_y, 1, at.to_c)

    def second(self):
        at = self.at
        self.need(at.chip_x, at.c, 1)
        self.push(at.chip_x, 1, at.to_c)
        self.need(at.chip_y, at.c, 0)
        self.push(at.chip_y, 0, at.to_c)
        for half in range(2):
            self.need(at.chip, 1 - at.c, half)
            self.need(at.chip_x, 1 - at.c, half)
            self.need(at.chip_y, 1 - at.c, half)

    def third(self):
        at = self.at
        for half in range(2):
            self.need(at.chip_d, at.c, half)
            self.push(at.chip_d, half, at.to_c)
        for half in range(2):
            self.need(at.chip_d, 1 - at.c, half)

    def finish(self):
        for one in self.sent:
            one.wait_send()


class Halo:
    def __init__(self, at, kv, rows, sems):
        self.at, self.kv, self.rows, self.sems = at, kv, rows, sems

    def piece(self, block, h):
        cols = pl.ds(pl.multiple_of(h * 256, 256), 256)
        return self.kv.at[pl.ds(block * self.rows, self.rows), cols]

    def on(self, h):
        return pltpu.make_async_remote_copy(
            src_ref=self.piece(2, h), dst_ref=self.piece(0, h),
            send_sem=self.sems.at[0, h], recv_sem=self.sems.at[1, h],
            device_id=self.at.after, device_id_type=MESH)

    def across(self, block, h):
        return pltpu.make_async_remote_copy(
            src_ref=self.piece(block, h), dst_ref=self.piece(1, h),
            send_sem=self.sems.at[2, h], recv_sem=self.sems.at[3, h],
            device_id=self.at.to_c, device_id_type=MESH)

    def start(self, h):
        @pl.when(self.at.chip < 3)
        def _():
            self.on(h).start()

        @pl.when(self.at.c == 0)
        def _():
            self.across(2, h).start()

    def need(self, h):
        at = self.at

        @pl.when(at.chip > 0)
        def _():
            self.on(h).wait_recv()

            @pl.when(at.c == 1)
            def _():
                self.across(0, h).start()

        @pl.when((at.chip > 0) | (at.c == 1))
        def _():
            self.across(0, h).wait_recv()

    def finish(self, h):
        at = self.at

        @pl.when(at.chip < 3)
        def _():
            self.on(h).wait_send()

        @pl.when((at.chip > 0) | (at.c == 0))
        def _():
            self.across(0, h).wait_send()


def kernel(x, wq, wk, wv, wo, gain_q, gain_k, cosine, sine, out,
           x_all, w_all, total, turned_x, o_all, mixed, kv, q, total_o,
           zs, zr, ks, kr, qs, qr, ms, mr, os, orr, hs, local):
    at = Place()
    depth, rows = x.shape
    nq, nk = wq.shape[1], wk.shape[1]
    features = wo.shape[0]
    heads = nk // 128
    shard = depth // 2
    device = at.chip * 2 + at.c
    mine = pl.ds(pl.multiple_of(device * shard, 16), shard)
    loads = [
        pltpu.make_async_copy(x, x_all.at[at.z], local.at[0]),
        pltpu.make_async_copy(wq, w_all.at[mine, pl.ds(0, nq)], local.at[1]),
        pltpu.make_async_copy(wk, w_all.at[mine, pl.ds(nq, nk)], local.at[2]),
        pltpu.make_async_copy(wv, w_all.at[mine, pl.ds(nq + nk, nk)], local.at[3]),
    ]
    load_o = pltpu.make_async_copy(wo, o_all.at[device], local.at[4])
    for load in loads:
        load.start()
    barrier(at)
    for load in loads:
        load.wait()
    load_o.start()
    half = rows // 2
    wide = features // 2

    def weight_part(low, width):
        def part(index, h):
            start = pl.multiple_of(index * shard + h * (shard // 2), 16)
            return w_all.at[pl.ds(start, shard // 2), pl.ds(low, width)]
        return part

    line = Line(at, lambda b, p: x_all.at[b, pl.ds(p * shard, shard)], zs, zr)
    line_m = Line(at, lambda b, p: mixed.at[b, :, pl.ds(p * 256, 256)], ms, mr)
    plane_k = Plane(at, weight_part(nq, 2 * nk), ks, kr)
    plane_q = Plane(at, weight_part(0, nq), qs, qr)
    plane_o = Plane(at, lambda i, h: o_all.at[i, pl.ds(h * wide, wide)], os, orr)
    halo = Halo(at, kv, rows, hs)

    def far(j):
        return (j - at.z == 3) | (at.z - j == 3)

    def project(j, p, low, high):
        turned_x[...] = x_all[j, p * shard:(p + 1) * shard, :].T
        start = pl.multiple_of((j * 2 + p) * shard, 16)

        @pl.loop(0, (high - low) // 256)
        def _(tile):
            cols = pl.ds(pl.multiple_of(low + tile * 256, 256), 256)
            total[:, cols] += jnp.dot(
                turned_x[...], w_all[pl.ds(start, shard), cols],
                preferred_element_type=jnp.float32)

    def project_some(which, parts, low, high):
        @pl.loop(0, 4)
        def _(j):
            @pl.when(which(j))
            def _():
                for p in parts:
                    project(j, p, low, high)

    line.start(0)
    plane_k.start()
    line.start(1)
    total[...] = jnp.zeros_like(total)
    total_o[...] = jnp.zeros_like(total_o)

    @pl.when(at.chip == 0)
    def _():
        kv[pl.ds(0, rows), :] = jnp.zeros((rows, 2 * nk), jnp.bfloat16)

        @pl.when(at.c == 0)
        def _():
            kv[pl.ds(rows, rows), :] = jnp.zeros((rows, 2 * nk), jnp.bfloat16)

    plane_k.first()
    plane_q.start()
    line.step(1, 0)
    plane_k.second()
    line.step(1, 1)
    line.step(2, 0)
    plane_k.third()
    line.step(2, 1)
    plane_q.first()
    project_some(lambda j: jnp.logical_not(far(j)), (0, 1), nq, nq + 2 * nk)
    plane_q.second()
    project_some(lambda j: jnp.logical_not(far(j) | (j == at.chip_d)), (0, 1), 0, nq)

    def head(col, gain):
        block = total[:, pl.ds(pl.multiple_of(col, 128), 128)]
        mean_square = jnp.mean(block * block, axis=-1, keepdims=True)
        normed = block * lax.rsqrt(mean_square + 1e-06) * gain
        turned = normed * cosine[...] + pltpu.roll(normed, 64, 1) * sine[...]
        return turned.astype(jnp.bfloat16)

    for part in range(2):
        line.step(3, part)
        project_some(far, (part,), nq, nq + 2 * nk)
    own = pl.ds(2 * rows, rows)

    @pl.loop(0, heads)
    def _(h):
        kv[own, pl.ds(pl.multiple_of(h * 256, 256), 128)] = head(nq + h * 128, gain_k[...])
        values = total[:, pl.ds(pl.multiple_of(nq + nk + h * 128, 128), 128)]
        kv[own, pl.ds(pl.multiple_of(h * 256 + 128, 128), 128)] = values.astype(jnp.bfloat16)
        halo.start(h)

    plane_q.third()
    project_some(lambda j: far(j) | (j == at.chip_d), (0, 1), 0, nq)

    @pl.loop(0, nq // 128)
    def _(h):
        q[:, pl.ds(pl.multiple_of(h * 128, 128), 128)] = head(h * 128, gain_q[...])

    span = half + 2 * rows
    for tile in range(2):
        query = lax.broadcasted_iota(jnp.int32, (half, span), 0)
        key = lax.broadcasted_iota(jnp.int32, (half, span), 1)
        low = 2 * rows - device * rows - tile * half
        valid = (key > query) & (key <= query + WINDOW_KEYS) & (key >= low)
        total[pl.ds(tile * half, half), 0:span] = jnp.where(valid, 0.0, -1e30)

    def attend_head(h):
        @pl.loop(0, 2)
        def _(tile):
            first = pl.multiple_of(tile * half, half)
            keys = kv[pl.ds(first, span), h * 256:h * 256 + 128]
            values = kv[pl.ds(first, span), h * 256 + 128:h * 256 + 256]
            for g in range(2):
                cols = slice((2 * h + g) * 128, (2 * h + g + 1) * 128)
                scores = lax.dot_general(
                    q[pl.ds(first, half), cols], keys, (((1,), (1,)), ((), ())),
                    preferred_element_type=jnp.float32)
                scores = scores + total[pl.ds(first, half), 0:span]
                top = jnp.max(scores, axis=-1, keepdims=True)
                weights = jnp.exp2((scores - top) * (query_scale * LOG2_E))
                inverse = 1.0 / jnp.sum(weights, axis=-1, keepdims=True)
                weights = (weights * inverse).astype(jnp.bfloat16)
                mixed[at.z, pl.ds(first, half), cols] = jnp.dot(
                    weights, values, preferred_element_type=jnp.float32).astype(jnp.bfloat16)

    for h in range(heads):
        halo.need(h)
        if h == heads - 1:
            load_o.wait()
            plane_o.start()
        attend_head(h)
        line_m.start(h)
        if h > 0:
            line_m.step(1, h - 1)

    def output(j, p):
        @pl.loop(0, 2)
        def _(tile):
            some = pl.ds(pl.multiple_of(tile * wide, 32), wide)
            total_o[some, :] += lax.dot_general(
                o_all[j * 2 + p, some, :], mixed[j, :, p * (nq // 2):(p + 1) * (nq // 2)],
                (((1,), (1,)), ((), ())), preferred_element_type=jnp.float32)

    line_m.step(1, heads - 1)
    line_m.step(2, 0)
    plane_o.first()
    line_m.step(2, 1)
    line_m.step(2, 2)
    plane_o.second()
    line_m.step(2, 3)
    plane_o.third()

    @pl.loop(0, 4)
    def _(j):
        @pl.when(jnp.logical_not(far(j)))
        def _():
            for p in range(2):
                output(j, p)

    for p in range(2):
        line_m.step(3, 2 * p)
        line_m.step(3, 2 * p + 1)

        @pl.loop(0, 4)
        def _(j):
            @pl.when(far(j))
            def _():
                output(j, p)

    out[...] = total_o[...].astype(jnp.bfloat16)
    line.finish(2)
    line_m.finish(heads)
    plane_k.finish()
    plane_q.finish()
    plane_o.finish()
    for h in range(heads):
        halo.finish(h)


def angles_of(positions):
    freqs = 10000.0 ** (-(jnp.arange(64, dtype=jnp.float32) * 2.0 / HEAD_SIZE))
    angles = positions.astype(jnp.float32)[:, None] * freqs[None, :]
    cosine, sine = jnp.cos(angles), jnp.sin(angles)
    return jnp.concatenate([cosine, cosine], 1), jnp.concatenate([-sine, sine], 1)


def fused(tokens, w_query, key_weight, value_weight, w_output, query_gain, key_gain):
    rows, depth = tokens.shape
    nq, nk = w_query.shape[1], key_weight.shape[1]
    features = w_output.shape[1]
    base = lax.axis_index(("seq", "row")) * rows
    cosine, sine = angles_of(base + jnp.arange(rows, dtype=jnp.int32))
    hbm = pl.BlockSpec(memory_space=pl.ANY)
    vmem = pl.BlockSpec(memory_space=pltpu.VMEM)
    bf16, dma = jnp.bfloat16, pltpu.SemaphoreType.DMA
    return pl.pallas_call(
        kernel,
        out_shape=jax.ShapeDtypeStruct((features, rows), bf16),
        in_specs=[hbm] * 5 + [vmem] * 4,
        out_specs=vmem,
        scratch_shapes=[
            pltpu.VMEM((4, depth, rows), bf16),
            pltpu.VMEM((4 * depth, nq + 2 * nk), bf16),
            pltpu.VMEM((rows, nq + 2 * nk), jnp.float32),
            pltpu.VMEM((rows, depth // 2), bf16),
            pltpu.VMEM((8, features, nq // 2), bf16),
            pltpu.VMEM((4, rows, nq), bf16),
            pltpu.VMEM((3 * rows, 2 * nk), bf16),
            pltpu.VMEM((rows, nq), bf16),
            pltpu.VMEM((features, rows), jnp.float32),
            dma((2, 4, 2)), dma((4, 2)),
            dma((SENDS,)), dma((8, 2)), dma((SENDS,)), dma((8, 2)),
            dma((2, 4, 4)), dma((4, 4)), dma((SENDS,)), dma((8, 2)),
            dma((4, 4)), dma((5,)),
        ],
        compiler_params=pltpu.CompilerParams(
            collective_id=0, has_side_effects=True, vmem_limit_bytes=62 * MIB),
    )(tokens.T, w_query, key_weight, value_weight, w_output.T,
      query_gain.reshape(1, HEAD_SIZE), key_gain.reshape(1, HEAD_SIZE), cosine, sine).T


def solution(mesh):
    small = dict(mesh.shape) == {"seq": 2, "row": 4, "col": 4}
    split = P(("seq", "row"), "col")
    return jax.shard_map(
        fused if small else shards,
        mesh=mesh,
        in_specs=(split, split, split, split, split, P(), P()),
        out_specs=split,
        check_vma=False,
    )
```

```python
import jax
import jax.numpy as jnp
from jax import lax
from jax.experimental import pallas as pl
from jax.experimental.pallas import tpu as pltpu
from jax.sharding import PartitionSpec as P

HEAD_SIZE = 128
WINDOW_KEYS = 1024


query_scale = 168.0 ** (-0.5)


def shifted(block, axis, distance):
    devices = range(lax.axis_size(axis))
    route = [(i - distance, i) for i in devices if i - distance in devices]
    return lax.ppermute(block, axis, route)


def head_norm(block, gain):
    mean_square = jnp.mean(block * block, axis=-1, keepdims=True)
    return block * lax.rsqrt(mean_square + 1e-06) * gain


def rotate(block, positions):
    half = block.shape[-1] // 2
    freqs = 10000.0 ** (-(jnp.arange(half, dtype=jnp.float32) * 2.0 / block.shape[-1]))
    angles = positions.astype(jnp.float32)[:, None] * freqs[None, :]
    cosine = jnp.cos(angles)[:, None, :]
    sine = jnp.sin(angles)[:, None, :]
    first = block[..., :half]
    second = block[..., half:]
    return jnp.concatenate(
        [first * cosine - second * sine, second * cosine + first * sine], axis=-1
    )


def attend(queries, key_states, value_states, qpos, kpos):
    rows = queries.shape[0]
    kv_heads = key_states.shape[1]
    grouped = queries.reshape(rows, kv_heads, 2, HEAD_SIZE)
    scores = (
        jnp.einsum("bhgd,khd->hgbk", grouped, key_states, preferred_element_type=jnp.float32)
        * query_scale
    )
    gap = qpos[:, None] - kpos[None, :]
    valid = (kpos[None, :] >= 0) & (gap >= 0) & (gap < WINDOW_KEYS)
    scores = jnp.where(valid[None, None], scores, -1e30)
    top = jnp.max(scores, axis=-1, keepdims=True)
    weights = jnp.exp(scores - top)
    weights = (weights / jnp.sum(weights, axis=-1, keepdims=True)).astype(jnp.bfloat16)
    mixed = jnp.einsum("hgbk,khd->bhgd", weights, value_states, preferred_element_type=jnp.float32)
    return mixed.astype(jnp.bfloat16).reshape(rows, kv_heads * 2 * HEAD_SIZE)


def shards(tokens, w_query, key_weight, value_weight, w_output, query_gain, key_gain):
    rows = tokens.shape[0]
    whole = lax.all_gather(tokens, "col", axis=1, tiled=True)
    columns = whole
    proj_q = jnp.dot(
        columns,
        lax.all_gather(w_query, ("seq", "row"), axis=0, tiled=True),
        preferred_element_type=jnp.float32,
    )
    projected_key = jnp.dot(
        columns,
        lax.all_gather(key_weight, ("seq", "row"), axis=0, tiled=True),
        preferred_element_type=jnp.float32,
    )
    proj_v = jnp.dot(
        columns,
        lax.all_gather(value_weight, ("seq", "row"), axis=0, tiled=True),
        preferred_element_type=jnp.float32,
    )
    base = lax.axis_index(("seq", "row")) * rows
    positions = base + jnp.arange(rows, dtype=jnp.int32)
    q_heads = proj_q.shape[1] // HEAD_SIZE
    kv_heads = projected_key.shape[1] // HEAD_SIZE
    queries = rotate(
        head_norm(proj_q.reshape(rows, q_heads, HEAD_SIZE), query_gain), positions
    ).astype(jnp.bfloat16)
    key_states = rotate(
        head_norm(projected_key.reshape(rows, kv_heads, HEAD_SIZE), key_gain), positions
    ).astype(jnp.bfloat16)
    key_flat = key_states.reshape(rows, kv_heads * HEAD_SIZE)
    value_flat = proj_v.astype(jnp.bfloat16)
    prior_one = shifted((key_flat, value_flat), ("seq", "row"), 1)
    prior_two = shifted((key_flat, value_flat), ("seq", "row"), 2)
    key_rows = jnp.concatenate([prior_two[0], prior_one[0], key_flat], axis=0).reshape(
        3 * rows, kv_heads, HEAD_SIZE
    )
    value_rows = jnp.concatenate([prior_two[1], prior_one[1], value_flat], axis=0).reshape(
        3 * rows, kv_heads, HEAD_SIZE
    )
    kpos = base - 2 * rows + jnp.arange(3 * rows, dtype=jnp.int32)
    mixed = attend(queries, key_rows, value_rows, positions, kpos)
    all_heads = lax.all_gather(mixed, "col", axis=1, tiled=True)
    columns = all_heads
    attended = jnp.dot(
        columns,
        lax.all_gather(w_output, ("seq", "row"), axis=0, tiled=True),
        preferred_element_type=jnp.float32,
    )
    return attended.astype(jnp.bfloat16)


MESH = pl.DeviceIdType.MESH
MIB = 1 << 20
SENDS = 14
LOG2_E = 1.4426950408889634


class Place:
    def __init__(self):
        self.y = lax.axis_index("seq")
        row = lax.axis_index("row")
        self.x, self.c = row // 2, row % 2
        self.z = lax.axis_index("col")
        self.to_x = {"seq": self.y, "row": (1 - self.x) * 2 + self.c, "col": self.z}
        self.to_y = {"seq": 1 - self.y, "row": row, "col": self.z}
        self.to_c = {"seq": self.y, "row": self.x * 2 + 1 - self.c, "col": self.z}
        self.up = {"seq": self.y, "row": row, "col": self.z + 1}
        self.down = {"seq": self.y, "row": row, "col": self.z - 1}
        self.to_d = {"seq": 1 - self.y, "row": (1 - self.x) * 2 + self.c, "col": self.z}
        self.chip = self.y * 2 + self.x
        after = (self.chip + 1) % 4
        self.after = {"seq": after // 2, "row": (after % 2) * 2 + self.c, "col": self.z}
        self.chip_x = self.y * 2 + 1 - self.x
        self.chip_y = (1 - self.y) * 2 + self.x
        self.chip_d = (1 - self.y) * 2 + 1 - self.x


def barrier(at):
    sem = pltpu.get_barrier_semaphore()
    for device in (at.to_x, at.to_y, at.to_c, at.to_d):
        pl.semaphore_signal(sem, inc=1, device_id=device, device_id_type=MESH)

    @pl.when(at.z < 3)
    def _():
        pl.semaphore_signal(sem, inc=1, device_id=at.up, device_id_type=MESH)

    @pl.when(at.z > 0)
    def _():
        pl.semaphore_signal(sem, inc=1, device_id=at.down, device_id_type=MESH)

    peers = 4 + (at.z < 3).astype(jnp.int32) + (at.z > 0).astype(jnp.int32)
    pl.semaphore_wait(sem, peers)


class Line:
    def __init__(self, at, part, send, recv):
        self.at, self.part, self.send, self.recv = at, part, send, recv

    def copy(self, block, part, way):
        piece = self.part(block, part)
        return pltpu.make_async_remote_copy(
            src_ref=piece, dst_ref=piece,
            send_sem=self.send.at[way, block, part], recv_sem=self.recv.at[block, part],
            device_id=self.at.up if way == 0 else self.at.down, device_id_type=MESH)

    def start(self, part):
        at = self.at

        @pl.when(at.z < 3)
        def _():
            self.copy(at.z, part, 0).start()

        @pl.when(at.z > 0)
        def _():
            self.copy(at.z, part, 1).start()

    def step(self, s, part):
        at = self.at

        @pl.when(at.z - s >= 0)
        def _():
            self.copy(at.z - s, part, 0).wait_recv()

            @pl.when(at.z < 3)
            def _():
                self.copy(at.z - s, part, 0).start()

        @pl.when(at.z + s <= 3)
        def _():
            self.copy(at.z + s, part, 1).wait_recv()

            @pl.when(at.z > 0)
            def _():
                self.copy(at.z + s, part, 1).start()

    def finish(self, parts):
        at = self.at
        for s in range(4):
            for part in range(parts):
                @pl.when((at.z - s >= 0) & (at.z < 3))
                def _():
                    self.copy(at.z - s, part, 0).wait_send()

                @pl.when((at.z + s <= 3) & (at.z > 0))
                def _():
                    self.copy(at.z + s, part, 1).wait_send()


class Plane:
    def __init__(self, at, part, send, recv):
        self.at, self.part, self.send, self.recv = at, part, send, recv
        self.sent = []

    def copy(self, chip, core, half, device, slot):
        piece = self.part(chip * 2 + core, half)
        return pltpu.make_async_remote_copy(
            src_ref=piece, dst_ref=piece,
            send_sem=self.send.at[slot], recv_sem=self.recv.at[chip * 2 + core, half],
            device_id=device, device_id_type=MESH)

    def push(self, chip, half, device):
        one = self.copy(chip, self.at.c, half, device, len(self.sent))
        one.start()
        self.sent.append(one)

    def need(self, chip, core, half):
        self.copy(chip, core, half, self.at.to_c, 0).wait_recv()

    def start(self):
        at = self.at
        self.push(at.chip, 0, at.to_x)
        self.push(at.chip, 1, at.to_y)
        self.push(at.chip, 1, at.to_x)
        self.push(at.chip, 0, at.to_y)
        self.push(at.chip, 0, at.to_c)
        self.push(at.chip, 1, at.to_c)

    def first(self):
        at = self.at
        self.need(at.chip_x, at.c, 0)
        self.push(at.chip_x, 0, at.to_y)
        self.push(at.chip_x, 0, at.to_c)
        self.need(at.chip_y, at.c, 1)
        self.push(at.chip_y, 1, at.to_x)
        self.push(at.chip_y, 1, at.to_c)

    def second(self):
        at = self.at
        self.need(at.chip_x, at.c, 1)
        self.push(at.chip_x, 1, at.to_c)
        self.need(at.chip_y, at.c, 0)
        self.push(at.chip_y, 0, at.to_c)
        for half in range(2):
            self.need(at.chip, 1 - at.c, half)
            self.need(at.chip_x, 1 - at.c, half)
            self.need(at.chip_y, 1 - at.c, half)

    def third(self):
        at = self.at
        for half in range(2):
            self.need(at.chip_d, at.c, half)
            self.push(at.chip_d, half, at.to_c)
        for half in range(2):
            self.need(at.chip_d, 1 - at.c, half)

    def finish(self):
        for one in self.sent:
            one.wait_send()


class Halo:
    def __init__(self, at, kv, rows, sems):
        self.at, self.kv, self.rows, self.sems = at, kv, rows, sems

    def piece(self, block, h):
        cols = pl.ds(pl.multiple_of(h * 256, 256), 256)
        return self.kv.at[pl.ds(block * self.rows, self.rows), cols]

    def on(self, h):
        return pltpu.make_async_remote_copy(
            src_ref=self.piece(2, h), dst_ref=self.piece(0, h),
            send_sem=self.sems.at[0, h], recv_sem=self.sems.at[1, h],
            device_id=self.at.after, device_id_type=MESH)

    def across(self, block, h):
        return pltpu.make_async_remote_copy(
            src_ref=self.piece(block, h), dst_ref=self.piece(1, h),
            send_sem=self.sems.at[2, h], recv_sem=self.sems.at[3, h],
            device_id=self.at.to_c, device_id_type=MESH)

    def start(self, h):
        @pl.when(self.at.chip < 3)
        def _():
            self.on(h).start()

        @pl.when(self.at.c == 0)
        def _():
            self.across(2, h).start()

    def need(self, h):
        at = self.at

        @pl.when(at.chip > 0)
        def _():
            self.on(h).wait_recv()

            @pl.when(at.c == 1)
            def _():
                self.across(0, h).start()

        @pl.when((at.chip > 0) | (at.c == 1))
        def _():
            self.across(0, h).wait_recv()

    def finish(self, h):
        at = self.at

        @pl.when(at.chip < 3)
        def _():
            self.on(h).wait_send()

        @pl.when((at.chip > 0) | (at.c == 0))
        def _():
            self.across(0, h).wait_send()


def kernel(x, wq, wk, wv, wo, gain_q, gain_k, cosine, sine, out,
           x_all, w_all, total, turned_x, o_all, mixed, kv, q, total_o, mask,
           zs, zr, ks, kr, qs, qr, ms, mr, os, orr, hs, local):
    at = Place()
    depth, rows = x.shape
    nq, nk = wq.shape[1], wk.shape[1]
    features = wo.shape[0]
    heads = nk // 128
    shard = depth // 2
    device = at.chip * 2 + at.c
    mine = pl.ds(pl.multiple_of(device * shard, 16), shard)
    loads = [
        pltpu.make_async_copy(x, x_all.at[at.z], local.at[0]),
        pltpu.make_async_copy(wq, w_all.at[mine, pl.ds(0, nq)], local.at[1]),
        pltpu.make_async_copy(wk, w_all.at[mine, pl.ds(nq, nk)], local.at[2]),
        pltpu.make_async_copy(wv, w_all.at[mine, pl.ds(nq + nk, nk)], local.at[3]),
    ]
    load_o = pltpu.make_async_copy(wo, o_all.at[device], local.at[4])
    for load in loads:
        load.start()
    barrier(at)
    for load in loads:
        load.wait()
    load_o.start()
    half = rows // 2
    wide = features // 2

    def weight_part(low, width):
        def part(index, h):
            start = pl.multiple_of(index * shard + h * (shard // 2), 16)
            return w_all.at[pl.ds(start, shard // 2), pl.ds(low, width)]
        return part

    line = Line(at, lambda b, p: x_all.at[b, pl.ds(p * shard, shard)], zs, zr)
    line_m = Line(at, lambda b, p: mixed.at[b, :, pl.ds(p * 256, 256)], ms, mr)
    plane_k = Plane(at, weight_part(nq, 2 * nk), ks, kr)
    plane_q = Plane(at, weight_part(0, nq), qs, qr)
    plane_o = Plane(at, lambda i, h: o_all.at[i, pl.ds(h * wide, wide)], os, orr)
    halo = Halo(at, kv, rows, hs)

    def far(j):
        return (j - at.z == 3) | (at.z - j == 3)

    def project(j, p, low, high):
        turned_x[...] = x_all[j, p * shard:(p + 1) * shard, :].T
        start = pl.multiple_of((j * 2 + p) * shard, 16)

        @pl.loop(0, (high - low) // 256)
        def _(tile):
            cols = pl.ds(pl.multiple_of(low + tile * 256, 256), 256)
            total[:, cols] += jnp.dot(
                turned_x[...], w_all[pl.ds(start, shard), cols],
                preferred_element_type=jnp.float32)

    def project_some(which, parts, low, high):
        @pl.loop(0, 4)
        def _(j):
            @pl.when(which(j))
            def _():
                for p in parts:
                    project(j, p, low, high)

    line.start(0)
    plane_k.start()
    line.start(1)
    total[...] = jnp.zeros_like(total)
    total_o[...] = jnp.zeros_like(total_o)

    @pl.when(at.chip == 0)
    def _():
        kv[pl.ds(0, rows), :] = jnp.zeros((rows, 2 * nk), jnp.bfloat16)

        @pl.when(at.c == 0)
        def _():
            kv[pl.ds(rows, rows), :] = jnp.zeros((rows, 2 * nk), jnp.bfloat16)

    plane_k.first()
    plane_q.start()
    line.step(1, 0)
    plane_k.second()
    line.step(1, 1)

    span = half + 2 * rows
    for tile in range(2):
        query = lax.broadcasted_iota(jnp.int32, (half, span), 0)
        key = lax.broadcasted_iota(jnp.int32, (half, span), 1)
        low = 2 * rows - device * rows - tile * half
        valid = (key > query) & (key <= query + WINDOW_KEYS) & (key >= low)
        mask[tile] = jnp.where(valid, 0.0, -1e30)

    line.step(2, 0)
    plane_k.third()
    line.step(2, 1)
    plane_q.first()
    project_some(lambda j: jnp.logical_not(far(j)), (0, 1), nq, nq + 2 * nk)
    plane_q.second()
    project_some(lambda j: jnp.logical_not(far(j) | (j == at.chip_d)), (0, 1), 0, nq)

    def head(col, gain):
        block = total[:, pl.ds(pl.multiple_of(col, 128), 128)]
        mean_square = jnp.mean(block * block, axis=-1, keepdims=True)
        normed = block * lax.rsqrt(mean_square + 1e-06) * gain
        turned = normed * cosine[...] + pltpu.roll(normed, 64, 1) * sine[...]
        return turned.astype(jnp.bfloat16)

    for part in range(2):
        line.step(3, part)
        project_some(far, (part,), nq, nq + 2 * nk)
    own = pl.ds(2 * rows, rows)

    @pl.loop(0, heads)
    def _(h):
        kv[own, pl.ds(pl.multiple_of(h * 256, 256), 128)] = head(nq + h * 128, gain_k[...])
        values = total[:, pl.ds(pl.multiple_of(nq + nk + h * 128, 128), 128)]
        kv[own, pl.ds(pl.multiple_of(h * 256 + 128, 128), 128)] = values.astype(jnp.bfloat16)
        halo.start(h)

    plane_q.third()
    project_some(lambda j: far(j) | (j == at.chip_d), (0, 1), 0, nq)

    def attend_head(h):
        @pl.loop(0, 2)
        def _(tile):
            first = pl.multiple_of(tile * half, half)
            keys = kv[pl.ds(first, span), h * 256:h * 256 + 128]
            values = kv[pl.ds(first, span), h * 256 + 128:h * 256 + 256]
            for g in range(2):
                cols = slice((2 * h + g) * 128, (2 * h + g + 1) * 128)
                scores = lax.dot_general(
                    q[pl.ds(first, half), cols], keys, (((1,), (1,)), ((), ())),
                    preferred_element_type=jnp.float32)
                scores = scores + mask[tile]
                top = jnp.max(scores, axis=-1, keepdims=True)
                weights = jnp.exp2((scores - top) * (query_scale * LOG2_E))
                inverse = 1.0 / jnp.sum(weights, axis=-1, keepdims=True)
                weights = (weights * inverse).astype(jnp.bfloat16)
                mixed[at.z, pl.ds(first, half), cols] = jnp.dot(
                    weights, values, preferred_element_type=jnp.float32).astype(jnp.bfloat16)

    for h in range(heads):
        for g in (2 * h, 2 * h + 1):
            q[:, g * 128:(g + 1) * 128] = head(g * 128, gain_q[...])
        halo.need(h)
        if h == heads - 1:
            load_o.wait()
            plane_o.start()
        attend_head(h)
        line_m.start(h)
        if h > 0:
            line_m.step(1, h - 1)

    def output(j, p):
        @pl.loop(0, 2)
        def _(tile):
            some = pl.ds(pl.multiple_of(tile * wide, 32), wide)
            total_o[some, :] += lax.dot_general(
                o_all[j * 2 + p, some, :], mixed[j, :, p * (nq // 2):(p + 1) * (nq // 2)],
                (((1,), (1,)), ((), ())), preferred_element_type=jnp.float32)

    line_m.step(1, heads - 1)
    line_m.step(2, 0)
    plane_o.first()
    line_m.step(2, 1)
    line_m.step(2, 2)
    plane_o.second()
    line_m.step(2, 3)
    plane_o.third()

    @pl.loop(0, 4)
    def _(j):
        @pl.when(jnp.logical_not(far(j)))
        def _():
            for p in range(2):
                output(j, p)

    for p in range(2):
        line_m.step(3, 2 * p)
        line_m.step(3, 2 * p + 1)

        @pl.loop(0, 4)
        def _(j):
            @pl.when(far(j))
            def _():
                output(j, p)

    out[...] = total_o[...].astype(jnp.bfloat16)
    line.finish(2)
    line_m.finish(heads)
    plane_k.finish()
    plane_q.finish()
    plane_o.finish()
    for h in range(heads):
        halo.finish(h)


def angles_of(positions):
    freqs = 10000.0 ** (-(jnp.arange(64, dtype=jnp.float32) * 2.0 / HEAD_SIZE))
    angles = positions.astype(jnp.float32)[:, None] * freqs[None, :]
    cosine, sine = jnp.cos(angles), jnp.sin(angles)
    return jnp.concatenate([cosine, cosine], 1), jnp.concatenate([-sine, sine], 1)


def fused(tokens, w_query, key_weight, value_weight, w_output, query_gain, key_gain):
    rows, depth = tokens.shape
    nq, nk = w_query.shape[1], key_weight.shape[1]
    features = w_output.shape[1]
    base = lax.axis_index(("seq", "row")) * rows
    cosine, sine = angles_of(base + jnp.arange(rows, dtype=jnp.int32))
    hbm = pl.BlockSpec(memory_space=pl.ANY)
    vmem = pl.BlockSpec(memory_space=pltpu.VMEM)
    bf16, dma = jnp.bfloat16, pltpu.SemaphoreType.DMA
    return pl.pallas_call(
        kernel,
        out_shape=jax.ShapeDtypeStruct((features, rows), bf16),
        in_specs=[hbm] * 5 + [vmem] * 4,
        out_specs=vmem,
        scratch_shapes=[
            pltpu.VMEM((4, depth, rows), bf16),
            pltpu.VMEM((4 * depth, nq + 2 * nk), bf16),
            pltpu.VMEM((rows, nq + 2 * nk), jnp.float32),
            pltpu.VMEM((rows, depth // 2), bf16),
            pltpu.VMEM((8, features, nq // 2), bf16),
            pltpu.VMEM((4, rows, nq), bf16),
            pltpu.VMEM((3 * rows, 2 * nk), bf16),
            pltpu.VMEM((rows, nq), bf16),
            pltpu.VMEM((features, rows), jnp.float32),
            pltpu.VMEM((2, rows // 2, rows // 2 + WINDOW_KEYS), jnp.float32),
            dma((2, 4, 2)), dma((4, 2)),
            dma((SENDS,)), dma((8, 2)), dma((SENDS,)), dma((8, 2)),
            dma((2, 4, 4)), dma((4, 4)), dma((SENDS,)), dma((8, 2)),
            dma((4, 4)), dma((5,)),
        ],
        compiler_params=pltpu.CompilerParams(
            collective_id=0, has_side_effects=True, vmem_limit_bytes=62 * MIB),
    )(tokens.T, w_query, key_weight, value_weight, w_output.T,
      query_gain.reshape(1, HEAD_SIZE), key_gain.reshape(1, HEAD_SIZE), cosine, sine).T


def solution(mesh):
    small = dict(mesh.shape) == {"seq": 2, "row": 4, "col": 4}
    split = P(("seq", "row"), "col")
    return jax.shard_map(
        fused if small else shards,
        mesh=mesh,
        in_specs=(split, split, split, split, split, P(), P()),
        out_specs=split,
        check_vma=False,
    )
```
